256 devices in a mesh: occ: 32 (over y_lo, z, core), virt: 8 (over x, y_hi).
Axes of the slice: x: 4, y: 4 (y_hi: 2, y_lo: 2; y = y_hi * 2 + y_lo), z: 8, core: 2. Of those that a mesh axis runs over, the one named last changes fastest.
Arguments:
- factors_alpha: float32 [32, 512, 2048], P('occ', 'virt'), may hold values from -0.8 to 0.8
- factors_beta: float32 [32, 512, 2048], P('occ', 'virt'), may hold values from -0.8 to 0.8
- occ_energy: float32 [32], replicated, may hold values from -2.5 to -0.4
- vir_energy: float32 [512], replicated, may hold values from 0.3 to 3
- occ_orbital: int32 [32], replicated, may hold values from 0 to 31, each once
Outputs:
- grad_alpha: float32 [32, 512, 2048], P('occ', 'virt')
- grad_beta: float32 [32, 512, 2048], P('occ', 'virt')
The draws below stay inside these ranges and needn't reach their ends.
Inputs may be any that keep to these rules, and one draw needn't show every extreme that they name: `occ_orbital`: each index 0 .. 31 appears exactly once.
All inputs are finite; a program needn't handle non-finite values.
Results may differ from the reference program's by a relative error of at most 0.0003.
Values sent between devices are 32-bit elements; how exact they have to be, the bound alone decides.
No kernel may reach another device: no remote copies, remote signals or barrier semaphores. Data moves between devices by JAX's collectives and lax.ppermute only.
A program may use at most 64 MiB of HBM per device.

```python
import jax
import jax.numpy as jnp
from jax import lax

NV = 512
NAUX = 2048
OCC_DEV = 1
REACH = 3
NOCC = 32


def shard_levels(stream_key, shape, split, least, top_value):
    def one(position, parts):
        steps = jax.random.uniform(jax.random.fold_in(jax.random.fold_in(stream_key, 6), position), (parts,), jnp.float32, least / len(split), top_value / len(split))
        return jnp.repeat(jnp.exp(steps), shape[position] // parts).reshape((-1,) + (1,) * (len(shape) - position - 1))

    level = one(*split[0])
    for cut in split[1:]:
        level = level * one(*cut)
    return level


def noise(rng, dims, width, bound, pieces=(), kind=jnp.bfloat16):
    gain = shard_levels(rng, dims, pieces, -0.22, 0.18) if pieces else 1.0
    result = jax.random.normal(rng, dims, jnp.float32) * width * gain
    return jnp.minimum(jnp.maximum(result, -bound), bound).astype(kind)


def setup_inputs(seed: int = 0) -> dict:
    seeds = jax.random.split(jax.random.key(seed), 6)
    factors_alpha = noise(seeds[0], (NOCC, NV, NAUX), 0.1, 0.8, ((0, 32), (1, 8)), jnp.float32)
    factors_beta = noise(seeds[1], (NOCC, NV, NAUX), 0.1, 0.8, ((0, 32), (1, 8)), jnp.float32)
    occ_energy = jnp.clip(jax.random.uniform(seeds[2], (NOCC,), jnp.float32, -2.5, -0.4), -2.5, -0.4)
    vir_energy = jnp.clip(jax.random.uniform(seeds[3], (NV,), jnp.float32, 0.3, 3.0), 0.3, 3.0)
    occ_orbital = jax.random.permutation(seeds[4], NOCC).astype(jnp.int32)
    return {"factors_alpha": factors_alpha, "factors_beta": factors_beta, "occ_energy": occ_energy, "vir_energy": vir_energy, "occ_orbital": occ_orbital}


def reference(factors_alpha, factors_beta, occ_energy, vir_energy, occ_orbital):
    e_occ = occ_energy[occ_orbital]
    groups = NOCC // OCC_DEV
    alpha_groups = factors_alpha.reshape(groups, OCC_DEV, NV, NAUX)
    beta_groups = factors_beta.reshape(groups, OCC_DEV, NV, NAUX)
    energy_groups = e_occ.reshape(groups, OCC_DEV)
    high = lax.Precision.HIGHEST

    def amplitudes(g, h):
        integrals = jnp.einsum("iap,jbp->iajb", alpha_groups[g], beta_groups[h], precision=high)
        denom = (energy_groups[g][:, None, None, None] - vir_energy[None, :, None, None]
                 + energy_groups[h][None, None, :, None] - vir_energy[None, None, None, :])
        return integrals / denom

    def alpha_side(g):
        total = jnp.zeros((OCC_DEV, NV, NAUX), jnp.float32)
        for offset in range(-REACH, REACH + 1):
            h = ((g + offset) % groups).astype(jnp.int32)
            total = total + jnp.einsum("iajb,jbp->iap", amplitudes(g, h), beta_groups[h], precision=high)
        return total

    def beta_side(h):
        total = jnp.zeros((OCC_DEV, NV, NAUX), jnp.float32)
        for offset in range(-REACH, REACH + 1):
            g = ((h + offset) % groups).astype(jnp.int32)
            total = total + jnp.einsum("iajb,iap->jbp", amplitudes(g, h), alpha_groups[g], precision=high)
        return total

    order = jnp.arange(groups, dtype=jnp.int32)
    grad_alpha = lax.map(alpha_side, order).reshape(NOCC, NV, NAUX)
    grad_beta = lax.map(beta_side, order).reshape(NOCC, NV, NAUX)
    return grad_alpha, grad_beta
```

```python
import jax
import jax.numpy as jnp
from jax import lax
from jax.sharding import PartitionSpec as P

NX, NY = 4, 2
HIGH = lax.Precision.HIGH


def shift_x(value, by):
    pairs = [(x * NY + y, ((x + by) % NX) * NY + y) for x in range(NX) for y in range(NY)]
    return lax.ppermute(value, "virt", pairs)


def swap_y(value):
    return lax.ppermute(value, "virt", [(v, v ^ 1) for v in range(NX * NY)])


def shift_occ(value, by):
    n = lax.axis_size("occ")
    return lax.ppermute(value, "occ", [(o, (o + by) % n) for o in range(n)])


def swap_core(value):
    n = lax.axis_size("occ")
    return lax.ppermute(value, "occ", [(o, o ^ 1) for o in range(n)])


def far(value):
    n = lax.axis_size("occ")
    pairs = [(o, (o + 3) % n if o % 2 else (o - 3) % n) for o in range(n)]
    return lax.ppermute(value, "occ", pairs)


def shards(factors_alpha, factors_beta, occ_energy, vir_energy, occ_orbital):
    own_a, own_b = factors_alpha[0], factors_beta[0]
    rows = own_a.shape[0]
    n_occ = occ_orbital.shape[0]
    here = lax.axis_index("occ")
    slab = lax.axis_index("virt")
    x, y = slab // NY, slab % NY

    orb = jnp.arange(n_occ, dtype=jnp.int32)
    orbital_energy = jnp.sum(
        jnp.where(occ_orbital[:, None] == orb[None, :], occ_energy[None, :], 0.0), axis=1
    )
    even = jnp.array([0, -2, 2, 1, -1, 3, -3], jnp.int32)
    odd = jnp.array([0, -2, 2, -1, -3, 1, 3], jnp.int32)
    visit = (here + jnp.where(here % 2 == 0, even, odd)) % n_occ
    pair_energy = jnp.sum(
        jnp.where(visit[:, None] == orb[None, :], orbital_energy[None, :], 0.0), axis=1
    )
    vir = vir_energy.reshape(NX, NY, rows)
    vir = jnp.concatenate([vir, vir[: NX - 1]], 0)
    vir = jnp.concatenate([vir, vir[:, :1]], 1)
    vir_a = lax.dynamic_slice(vir, (x, y, 0), (NX, NY, rows)).transpose(1, 0, 2)
    vir_b = lax.dynamic_slice_in_dim(vir_energy, slab * rows, rows)
    col = (pair_energy[0] + pair_energy[:, None] - vir_b[None, :]).reshape(1, -1)

    b_down = shift_occ(own_b, 2)
    b_up = shift_occ(own_b, -2)
    a_1 = shift_x(own_a, -1)
    a_3 = shift_x(own_a, 1)
    a_0y = swap_y(own_a)
    b_far = far(own_b)
    a_2 = shift_x(own_a, 2)
    near = jnp.concatenate([own_b, b_down, b_up], 0)
    b_flip = swap_core(near)
    a_1y = swap_y(a_1)
    a_3y = swap_y(a_3)
    a_2y = swap_y(a_2)
    beta = jnp.concatenate([near, b_flip, b_far], 0)
    alpha0 = jnp.concatenate([own_a, a_1, a_2, a_3], 0)
    alpha1 = jnp.concatenate([a_0y, a_1y, a_2y, a_3y], 0)

    def amps(alpha, v):
        integrals = lax.dot_general(alpha, beta, (((1,), (1,)), ((), ())), precision=HIGH)
        return integrals / (col - v.reshape(-1, 1))

    def dot(p, q):
        return lax.dot_general(p, q, (((1,), (0,)), ((), ())), precision=HIGH)

    def dot_t(p, q):
        return lax.dot_general(p, q, (((0,), (0,)), ((), ())), precision=HIGH)

    t_0 = amps(alpha0, vir_a[0])
    t_1 = amps(alpha1, vir_a[1])
    g_1 = dot(t_1, beta).reshape(NX, rows, -1)
    back = {d: swap_y(g_1[d]) for d in (2, 1, 3, 0)}
    gb = dot_t(t_0, alpha0) + dot_t(t_1, alpha1)
    g_0 = dot(t_0, beta).reshape(NX, rows, -1)

    gb_far = far(gb[6 * rows :])
    sums = gb[: 3 * rows] + swap_core(gb[3 * rows : 6 * rows])
    grad_beta = (
        sums[:rows]
        + shift_occ(sums[rows : 2 * rows], -2)
        + shift_occ(sums[2 * rows :], 2)
        + gb_far
    )
    h = {d: g_0[d] + back[d] for d in (2, 1, 3, 0)}
    grad_alpha = h[0] + shift_x(h[2], 2) + shift_x(h[1], 1) + shift_x(h[3], -1)
    return (grad_alpha[None], grad_beta[None])


def solution(mesh):
    return jax.shard_map(
        shards,
        mesh=mesh,
        in_specs=(P("occ", "virt", None), P("occ", "virt", None), P(), P(), P()),
        out_specs=(P("occ", "virt", None), P("occ", "virt", None)),
        check_vma=False,
    )
```

```python
import jax
import jax.numpy as jnp
from jax import lax
from jax.experimental import pallas as pl
from jax.experimental.pallas import tpu as pltpu
from jax.sharding import PartitionSpec as P


NX, NY = 4, 2
HIGH = lax.Precision.HIGH


def shift_x(value, by):
    pairs = [(x * NY + y, ((x + by) % NX) * NY + y) for x in range(NX) for y in range(NY)]
    return lax.ppermute(value, "virt", pairs)


def swap_y(value):
    return lax.ppermute(value, "virt", [(v, v ^ 1) for v in range(NX * NY)])


def shift_occ(value, by):
    n = lax.axis_size("occ")
    return lax.ppermute(value, "occ", [(o, (o + by) % n) for o in range(n)])


def swap_core(value):
    n = lax.axis_size("occ")
    return lax.ppermute(value, "occ", [(o, o ^ 1) for o in range(n)])


def far(value):
    n = lax.axis_size("occ")
    pairs = [(o, (o + 3) % n if o % 2 else (o - 3) % n) for o in range(n)]
    return lax.ppermute(value, "occ", pairs)


def split(value, sizes):
    def kernel(value_ref, *out_refs):
        at = 0
        for size, out_ref in zip(sizes, out_refs):
            out_ref[...] = value_ref[at : at + size, :]
            at += size

    whole = pl.BlockSpec(memory_space=pltpu.VMEM)
    return pl.pallas_call(
        kernel,
        out_shape=[pltpu.VMEM((n, value.shape[1]), value.dtype) for n in sizes],
        in_specs=[whole],
        out_specs=[whole] * len(sizes),
        compiler_params=pltpu.CompilerParams(vmem_limit_bytes=1 << 20),
        cost_estimate=pl.CostEstimate(
            flops=0, bytes_accessed=2 * value.size * 4, transcendentals=0
        ),
    )(pltpu.with_memory_space_constraint(value, pltpu.VMEM))


def shards(factors_alpha, factors_beta, occ_energy, vir_energy, occ_orbital):
    own_a, own_b = factors_alpha[0], factors_beta[0]
    rows = own_a.shape[0]
    n_occ = occ_orbital.shape[0]
    here = lax.axis_index("occ")
    slab = lax.axis_index("virt")
    x, y = slab // NY, slab % NY

    orb = jnp.arange(n_occ, dtype=jnp.int32)
    orbital_energy = jnp.sum(
        jnp.where(occ_orbital[:, None] == orb[None, :], occ_energy[None, :], 0.0), axis=1
    )
    even = jnp.array([0, -2, 2, 1, -1, 3, -3], jnp.int32)
    odd = jnp.array([0, -2, 2, -1, -3, 1, 3], jnp.int32)
    visit = (here + jnp.where(here % 2 == 0, even, odd)) % n_occ
    pair_energy = jnp.sum(
        jnp.where(visit[:, None] == orb[None, :], orbital_energy[None, :], 0.0), axis=1
    )
    vir = vir_energy.reshape(NX, NY, rows)
    vir = jnp.concatenate([vir, vir[: NX - 1]], 0)
    vir = jnp.concatenate([vir, vir[:, :1]], 1)
    vir_a = lax.dynamic_slice(vir, (x, y, 0), (NX, NY, rows)).transpose(1, 0, 2)
    vir_b = lax.dynamic_slice_in_dim(vir_energy, slab * rows, rows)
    col = (pair_energy[0] + pair_energy[:, None] - vir_b[None, :]).reshape(1, -1)

    a_2 = shift_x(own_a, 2)
    a_0y = swap_y(own_a)
    a_1 = shift_x(own_a, -1)
    a_3 = shift_x(own_a, 1)
    b_down = shift_occ(own_b, 2)
    b_up = shift_occ(own_b, -2)
    b_far = far(own_b)
    near = jnp.concatenate([own_b, b_down, b_up], 0)
    b_flip = swap_core(near)
    a_1y = shift_x(a_0y, -1)
    a_3y = shift_x(a_0y, 1)
    a_2y = swap_y(a_2)
    beta = jnp.concatenate([near, b_flip, b_far], 0)

    def group(blocks, energies):
        alpha = jnp.concatenate(blocks, 0)
        v = jnp.concatenate(energies, 0).reshape(-1, 1)
        integrals = lax.dot_general(
            alpha, beta, (((1,), (1,)), ((), ())), precision=HIGH
        )
        t = integrals / (col - v)
        g = lax.dot_general(t, beta, (((1,), (0,)), ((), ())), precision=HIGH)
        b = lax.dot_general(t, alpha, (((0,), (0,)), ((), ())), precision=HIGH)
        return split(g, [rows] * len(blocks)), b

    g_0, gb_0 = group([own_a, a_1, a_2, a_3], list(vir_a[0]))
    g_1, gb_1 = group([a_0y, a_1y, a_2y, a_3y], list(vir_a[1]))
    in_1 = shift_x(g_1[1], 1)
    in_3 = shift_x(g_1[3], -1)
    in_2 = swap_y(g_1[2])
    out_1 = shift_x(g_0[1], 1)
    out_3 = shift_x(g_0[3], -1)
    gb = split(gb_0 + gb_1, [3 * rows, 3 * rows, rows])

    gb_near = swap_core(gb[1])
    gb_far = far(gb[2])
    sums = split(gb[0] + gb_near, [rows] * 3)
    gb_down = shift_occ(sums[1], -2)
    gb_up = shift_occ(sums[2], 2)
    across = swap_y(g_1[0] + in_1 + in_3)
    out_2 = shift_x(g_0[2] + in_2, 2)
    grad_alpha = g_0[0] + out_1 + out_3 + across + out_2
    grad_beta = sums[0] + gb_down + gb_up + gb_far
    return (grad_alpha[None], grad_beta[None])


def solution(mesh):
    return jax.shard_map(
        shards,
        mesh=mesh,
        in_specs=(P("occ", "virt", None), P("occ", "virt", None), P(), P(), P()),
        out_specs=(P("occ", "virt", None), P("occ", "virt", None)),
        check_vma=False,
    )
```

```python
import jax
import jax.numpy as jnp
from jax import lax
from jax.experimental import pallas as pl
from jax.experimental.pallas import tpu as pltpu
from jax.sharding import PartitionSpec as P


NX, NY = 4, 2
HIGH = lax.Precision.HIGH


def shift_x(value, by):
    pairs = [(x * NY + y, ((x + by) % NX) * NY + y) for x in range(NX) for y in range(NY)]
    return lax.ppermute(value, "virt", pairs)


def swap_y(value):
    return lax.ppermute(value, "virt", [(v, v ^ 1) for v in range(NX * NY)])


def shift_occ(value, by):
    n = lax.axis_size("occ")
    return lax.ppermute(value, "occ", [(o, (o + by) % n) for o in range(n)])


def swap_core(value):
    n = lax.axis_size("occ")
    return lax.ppermute(value, "occ", [(o, o ^ 1) for o in range(n)])


def far_pairs(n):
    half = n // 2
    direct, hop, rest = [], [], []
    for o in range(n):
        to = (o + 3) % n if o % 2 else (o - 3) % n
        if o % half in (half - 3, 2):
            hop.append((o, (o + half) % n))
            rest.append(((o + half) % n, to))
        else:
            direct.append((o, to))
    return direct, hop, rest


def neighbours(n):
    return [(o, (o + 1) % n if o % 2 else (o - 1) % n) for o in range(n)]


def along_occ(value, pairs):
    return lax.ppermute(value, "occ", pairs)


def split(value, sizes):
    def kernel(value_ref, *out_refs):
        at = 0
        for size, out_ref in zip(sizes, out_refs):
            out_ref[...] = value_ref[at : at + size, :]
            at += size

    whole = pl.BlockSpec(memory_space=pltpu.VMEM)
    return pl.pallas_call(
        kernel,
        out_shape=[pltpu.VMEM((n, value.shape[1]), value.dtype) for n in sizes],
        in_specs=[whole],
        out_specs=[whole] * len(sizes),
        compiler_params=pltpu.CompilerParams(vmem_limit_bytes=1 << 20),
        cost_estimate=pl.CostEstimate(
            flops=0, bytes_accessed=2 * value.size * 4, transcendentals=0
        ),
    )(pltpu.with_memory_space_constraint(value, pltpu.VMEM))


def fold(own, partner, far):
    rows = far.shape[0]

    def kernel(own_ref, partner_ref, far_ref, here_ref, down_ref, up_ref):
        odd = lax.rem(lax.axis_index("occ"), 2) == 1
        passed = far_ref[...]
        nothing = jnp.zeros_like(passed)
        here_ref[...] = own_ref[:rows, :] + partner_ref[:rows, :]
        down = own_ref[rows : 2 * rows, :] + partner_ref[rows : 2 * rows, :]
        up = own_ref[2 * rows :, :] + partner_ref[2 * rows :, :]
        down_ref[...] = down + jnp.where(odd, passed, nothing)
        up_ref[...] = up + jnp.where(odd, nothing, passed)

    whole = pl.BlockSpec(memory_space=pltpu.VMEM)
    return pl.pallas_call(
        kernel,
        out_shape=[pltpu.VMEM(far.shape, far.dtype)] * 3,
        in_specs=[whole] * 3,
        out_specs=[whole] * 3,
        compiler_params=pltpu.CompilerParams(vmem_limit_bytes=1 << 20),
        cost_estimate=pl.CostEstimate(
            flops=4 * own.size, bytes_accessed=8 * own.size, transcendentals=0
        ),
    )(*(pltpu.with_memory_space_constraint(v, pltpu.VMEM) for v in (own, partner, far)))


def shards(factors_alpha, factors_beta, occ_energy, vir_energy, occ_orbital):
    own_a, own_b = factors_alpha[0], factors_beta[0]
    rows = own_a.shape[0]
    n_occ = occ_orbital.shape[0]
    here = lax.axis_index("occ")
    slab = lax.axis_index("virt")
    x, y = slab // NY, slab % NY

    orb = jnp.arange(n_occ, dtype=jnp.int32)
    orbital_energy = jnp.sum(
        jnp.where(occ_orbital[:, None] == orb[None, :], occ_energy[None, :], 0.0), axis=1
    )
    even = jnp.array([0, -2, 2, 1, -1, 3, -3], jnp.int32)
    odd = jnp.array([0, -2, 2, -1, -3, 1, 3], jnp.int32)
    visit = (here + jnp.where(here % 2 == 0, even, odd)) % n_occ
    pair_energy = jnp.sum(
        jnp.where(visit[:, None] == orb[None, :], orbital_energy[None, :], 0.0), axis=1
    )
    vir = vir_energy.reshape(NX, NY, rows)
    vir = jnp.concatenate([vir, vir[: NX - 1]], 0)
    vir = jnp.concatenate([vir, vir[:, :1]], 1)
    vir_a = lax.dynamic_slice(vir, (x, y, 0), (NX, NY, rows)).transpose(1, 0, 2)
    vir_b = lax.dynamic_slice_in_dim(vir_energy, slab * rows, rows)
    col = (pair_energy[0] + pair_energy[:, None] - vir_b[None, :]).reshape(1, -1)

    direct, hop, rest = far_pairs(lax.axis_size("occ"))

    a_2 = shift_x(own_a, 2)
    a_0y = swap_y(own_a)
    a_1 = shift_x(own_a, -1)
    a_3 = shift_x(own_a, 1)
    b_down = shift_occ(own_b, 2)
    b_up = shift_occ(own_b, -2)
    b_far = along_occ(own_b, direct)
    b_hop = along_occ(own_b, hop)
    b_rest = along_occ(b_hop, rest)
    near = jnp.concatenate([own_b, b_down, b_up], 0)
    b_flip = swap_core(near)
    a_1y = shift_x(a_0y, -1)
    a_3y = shift_x(a_0y, 1)
    a_2y = swap_y(a_2)
    beta = jnp.concatenate([near, b_flip, b_far + b_rest], 0)

    def group(blocks, energies):
        alpha = jnp.concatenate(blocks, 0)
        v = jnp.concatenate(energies, 0).reshape(-1, 1)
        integrals = lax.dot_general(
            alpha, beta, (((1,), (1,)), ((), ())), precision=HIGH
        )
        t = integrals / (col - v)
        g = lax.dot_general(t, beta, (((1,), (0,)), ((), ())), precision=HIGH)
        b = lax.dot_general(t, alpha, (((0,), (0,)), ((), ())), precision=HIGH)
        return split(g, [rows] * len(blocks)), b

    g_0, gb_0 = group([own_a, a_1, a_2, a_3], list(vir_a[0]))
    g_1, gb_1 = group([a_0y, a_1y, a_2y, a_3y], list(vir_a[1]))
    in_1 = shift_x(g_1[1], 1)
    in_3 = shift_x(g_1[3], -1)
    in_2 = swap_y(g_1[2])
    out_1 = shift_x(g_0[1], 1)
    out_3 = shift_x(g_0[3], -1)
    gb = split(gb_0 + gb_1, [3 * rows, 3 * rows, rows])

    gb_near = swap_core(gb[1])
    gb_far = along_occ(gb[2], neighbours(lax.axis_size("occ")))
    sums = fold(gb[0], gb_near, gb_far)
    gb_down = shift_occ(sums[1], -2)
    gb_up = shift_occ(sums[2], 2)
    across = swap_y(g_1[0] + in_1 + in_3)
    out_2 = shift_x(g_0[2] + in_2, 2)
    grad_alpha = g_0[0] + out_1 + out_3 + across + out_2
    grad_beta = sums[0] + gb_down + gb_up
    return (grad_alpha[None], grad_beta[None])


def solution(mesh):
    return jax.shard_map(
        shards,
        mesh=mesh,
        in_specs=(P("occ", "virt", None), P("occ", "virt", None), P(), P(), P()),
        out_specs=(P("occ", "virt", None), P("occ", "virt", None)),
        check_vma=False,
    )
```
